32 devices in a mesh: group: 4 (over y, core), owner: 8 (over z, x).
Axes of the slice: x: 2, y: 2, z: 4, core: 2. Of those that a mesh axis runs over, the one named last changes fastest.
Arguments:
- queries: bfloat16 [2048, 4096], P(('group', 'owner')), may hold values from -0.099609375 to 0.099609375
- passages: bfloat16 [2048, 4096], P(('group', 'owner')), may hold values from -0.099609375 to 0.099609375
- send_order: int32 [32, 64], P(('group', 'owner')), may hold values from 0 to 63, each once within a row
- neg_rows: int32 [32, 8], P(('group', 'owner')), may hold values from 0 to 63
Outputs:
- query_grad: bfloat16 [2048, 4096], P(('group', 'owner'))
- passage_grad: bfloat16 [2048, 4096], P(('group', 'owner'))
- row_loss: float32 [2048], P(('group', 'owner'))
The draws below stay inside these ranges and needn't reach their ends.
Inputs may be any that keep to these rules, and one draw needn't show every extreme that they name: `send_order`: each row is a permutation of 0 .. 63. `neg_rows`: rows of the device's cluster, repeats allowed.
All inputs are finite; a program needn't handle non-finite values.
Results may differ from the reference program's by a relative error of at most 0.0053.
Values may be sent and summed in bfloat16 or wider, within the bound.
A program may use at most 64 MiB of HBM per device.

```python
import jax
import jax.numpy as jnp
from jax import lax

D = 4096
ROWS = 64
NEG = 8
SHARDS = 32
TOKENS = 2048
N_GROUP = 4
N_OWNER = 8


def set_ends(result, rng, smallest, high):
    longest = result.shape.index(max(result.shape))
    spots = []
    for shift in (0, 1):
        where = [jax.random.randint(jax.random.fold_in(rng, axis), (), 0, length) for axis, length in enumerate(result.shape)]
        where[longest] = (where[longest] + shift) % result.shape[longest]
        spots.append(tuple(where))
    return result.at[spots[0]].set(smallest).at[spots[1]].set(high)


def level_of(own_key, dims, pieces, least, largest):
    def one(dim, blocks):
        draws = jax.random.uniform(jax.random.fold_in(jax.random.fold_in(own_key, 6), dim), (blocks,), jnp.float32, least / len(pieces), largest / len(pieces))
        return jnp.repeat(jnp.exp(draws), dims[dim] // blocks).reshape((-1,) + (1,) * (len(dims) - dim - 1))

    gain = one(*pieces[0])
    for cut in pieces[1:]:
        gain = gain * one(*cut)
    return gain


def scatter_about(stream_key, shape, width, reach, shards=(), kind=jnp.bfloat16):
    level = level_of(stream_key, shape, shards, -0.22, 0.18) if shards else 1.0
    array = jax.random.normal(stream_key, shape, jnp.float32) * width * level
    return jnp.minimum(jnp.maximum(array, -reach), reach).astype(kind)


def setup_inputs(seed: int = 0) -> dict:
    arg_keys = jax.random.split(jax.random.key(seed), 5)
    return {
        "queries": scatter_about(arg_keys[0], (TOKENS, D), 0.015625, 0.099609375, ((0, 32),)),
        "passages": scatter_about(arg_keys[1], (TOKENS, D), 0.015625, 0.099609375, ((0, 32),)),
        "send_order": jax.vmap(lambda own: jax.random.permutation(own, ROWS))(jax.random.split(arg_keys[2], SHARDS)).reshape((SHARDS, ROWS)).astype(jnp.int32),
        "neg_rows": set_ends(jax.random.randint(arg_keys[3], (SHARDS, NEG), 0, ROWS), jax.random.fold_in(arg_keys[3], 1), 0, ROWS - 1).astype(jnp.int32),
    }


logit_divisor = 0.05
epsilon = 1e-06

def normalize_rows(values):
    values_f = values.astype(jnp.float32)
    row_norm = jnp.sqrt(lax.optimization_barrier(jnp.sum(values_f * values_f, axis=-1, keepdims=True)) + epsilon)
    return (values_f / row_norm, row_norm)

def unnormalize_grad(grad_in, unit_vals, row_norm):
    inner = lax.optimization_barrier(jnp.sum(unit_vals * grad_in, axis=-1, keepdims=True))
    return (grad_in - unit_vals * inner) / row_norm

def take_rows(table, index_rows):
    return table[index_rows]

def put_rows(index_rows, values):
    return jnp.zeros_like(values).at[index_rows].set(values)

def add_rows(table, index_rows, values):
    return table.at[index_rows].add(values)

def to_clusters(data, send_perm):
    grid = data.reshape(N_GROUP, N_OWNER, ROWS, D)
    sent = jax.vmap(jax.vmap(take_rows))(grid, send_perm.reshape(N_GROUP, N_OWNER, ROWS))
    per_peer = ROWS // N_OWNER
    sent = sent.reshape(N_GROUP, N_OWNER, N_OWNER, per_peer, D)
    return jnp.transpose(sent, (0, 2, 1, 3, 4)).reshape(N_GROUP, N_OWNER, ROWS, D)

def from_clusters(owned, send_perm):
    per_peer = ROWS // N_OWNER
    back = owned.reshape(N_GROUP, N_OWNER, N_OWNER, per_peer, D)
    back = jnp.transpose(back, (0, 2, 1, 3, 4)).reshape(N_GROUP, N_OWNER, ROWS, D)
    placed = jax.vmap(jax.vmap(put_rows))(send_perm.reshape(N_GROUP, N_OWNER, ROWS), back)
    return placed.reshape(N_GROUP * N_OWNER * ROWS, D)

def per_owner(inputs):
    owner_q, owner_p, owner_neg = inputs
    q_unit, q_norm = normalize_rows(owner_q)
    p_unit, p_norm = normalize_rows(owner_p)
    query_brain_float = q_unit.astype(jnp.bfloat16)
    passage_brain_float = p_unit.astype(jnp.bfloat16)
    picked = jax.vmap(take_rows)(owner_p, owner_neg).reshape(N_GROUP * NEG, D)
    n_unit, n_norm = normalize_rows(picked)
    negative_brain_float = n_unit.astype(jnp.bfloat16)
    distractor_fp32 = negative_brain_float.astype(jnp.float32)
    exact_matmul_mode = lax.Precision.HIGHEST

    def one_group(q_one, p_one, group_id):
        question_fp32 = q_one.astype(jnp.float32)
        document_fp32 = p_one.astype(jnp.float32)
        within_group_similarity = jnp.einsum('oa,ra->or', question_fp32, document_fp32, precision=exact_matmul_mode) / logit_divisor
        distractor_similarity = jnp.einsum('oa,ra->or', question_fp32, distractor_fp32, precision=exact_matmul_mode) / logit_divisor
        keep_mask = (jnp.arange(N_GROUP * NEG) // NEG != group_id).astype(jnp.float32)
        e_loc = jnp.exp(within_group_similarity)
        e_neg = jnp.exp(distractor_similarity) * keep_mask[None, :]
        denom_sum = lax.optimization_barrier(jnp.sum(e_loc, axis=1)) + lax.optimization_barrier(jnp.sum(e_neg, axis=1))
        loss_rows = jnp.log(denom_sum) - jnp.diagonal(within_group_similarity)
        within_group_derivative = (e_loc / denom_sum[:, None] - jnp.eye(ROWS, dtype=jnp.float32)).astype(jnp.bfloat16).astype(jnp.float32)
        distractor_derivative = (e_neg / denom_sum[:, None]).astype(jnp.bfloat16).astype(jnp.float32)
        question_change = (jnp.einsum('ly,yr->lr', within_group_derivative, document_fp32, precision=exact_matmul_mode) + jnp.einsum('ly,yr->lr', distractor_derivative, distractor_fp32, precision=exact_matmul_mode)) / logit_divisor
        document_change = jnp.einsum('un,uc->nc', within_group_derivative, question_fp32, precision=exact_matmul_mode) / logit_divisor
        distractor_change = jnp.einsum('un,uc->nc', distractor_derivative, question_fp32, precision=exact_matmul_mode) / logit_divisor
        term_n = lax.optimization_barrier(distractor_change.astype(jnp.bfloat16)).astype(jnp.float32)
        return (loss_rows, question_change, document_change, term_n)
    loss_rows, question_change, document_change, distractor_change = jax.vmap(one_group)(query_brain_float, passage_brain_float, jnp.arange(N_GROUP))
    d_n_sum = lax.optimization_barrier(jnp.sum(distractor_change, axis=0)).reshape(N_GROUP, NEG, D)
    document_change = jax.vmap(add_rows)(document_change, owner_neg, d_n_sum)
    grad_q = unnormalize_grad(question_change, q_unit, q_norm).astype(jnp.bfloat16)
    grad_p = unnormalize_grad(document_change, p_unit, p_norm).astype(jnp.bfloat16)
    return (loss_rows, grad_q, grad_p)

def reference(queries, passages, send_order, neg_rows):
    owned_q = to_clusters(queries, send_order)
    owned_p = to_clusters(passages, send_order)
    neg_grid = neg_rows.reshape(N_GROUP, N_OWNER, NEG)
    loss_rows, grad_q, grad_p = lax.map(per_owner, (jnp.transpose(owned_q, (1, 0, 2, 3)), jnp.transpose(owned_p, (1, 0, 2, 3)), jnp.transpose(neg_grid, (1, 0, 2))))
    grad_q = jnp.transpose(grad_q, (1, 0, 2, 3))
    grad_p = jnp.transpose(grad_p, (1, 0, 2, 3))
    row_loss = jnp.transpose(loss_rows, (1, 0, 2)).reshape(N_GROUP * N_OWNER * ROWS)
    return (from_clusters(grad_q, send_order), from_clusters(grad_p, send_order), row_loss)
```

```python
import functools

import jax
import jax.numpy as jnp
from jax import lax
from jax.experimental import pallas as pl
from jax.experimental.pallas import tpu as pltpu
from jax.sharding import PartitionSpec as P

logit_scale = 1.0 / 0.05
epsilon = 1e-06
MESH = pl.DeviceIdType.MESH
f32, bf16 = jnp.float32, jnp.bfloat16


def xor(a, b, size):
    out, bit = 0, 1
    while bit < size:
        out = out + ((a // bit + b // bit) % 2) * bit
        bit *= 2
    return out


def dot(a, b, dims=((1,), (0,))):
    return lax.dot_general(a, b, (dims, ((), ())), preferred_element_type=f32)


def kernel(
    owners, groups, step_peers,
    q_ref, p_ref, send_col, send_row, neg_col, neg_row,
    q_out, p_out, loss_out,
    sent, owned, keys, qh, coef, dp, negs, term, term_in, stage, back,
    send_sem, recv_sem, gsend_sem, grecv_sem,
):
    rows, width = q_ref.shape
    c = rows // owners
    n_neg = neg_col.shape[0]
    n_all = groups * n_neg
    steps = owners // step_peers
    span = step_peers * c
    g, o = lax.axis_index("group"), lax.axis_index("owner")
    my_step = o // step_peers

    barrier = pltpu.get_barrier_semaphore()

    @pl.loop(1, owners)
    def _(k):
        pl.semaphore_signal(barrier, inc=1, device_id=(g, xor(o, k, owners)), device_id_type=MESH)

    @pl.loop(1, groups)
    def _(k):
        pl.semaphore_signal(barrier, inc=1, device_id=(xor(g, k, groups), o), device_id_type=MESH)

    pick = (send_col[...] == lax.broadcasted_iota(jnp.int32, (rows, rows), 1)).astype(f32).astype(bf16)
    sent[0] = dot(pick, p_ref[...]).reshape(owners, c, width).astype(bf16)
    sent[1] = dot(pick, q_ref[...]).reshape(owners, c, width).astype(bf16)
    pl.semaphore_wait(barrier, owners + groups - 2)

    def copy_in(kind, src_slot, dst_slot, peer):
        return pltpu.make_async_remote_copy(
            sent.at[kind, src_slot], owned.at[kind, dst_slot],
            send_sem.at[kind, src_slot], recv_sem.at[kind, dst_slot],
            device_id=(g, peer), device_id_type=MESH)

    def copy_back(kind, src_slot, dst_slot, peer):
        return pltpu.make_async_remote_copy(
            stage.at[kind, src_slot], back.at[kind, dst_slot],
            send_sem.at[2 + kind, src_slot], recv_sem.at[2 + kind, dst_slot],
            device_id=(g, peer), device_id_type=MESH)

    def copy_neg(slot, send_slot, peer):
        return pltpu.make_async_remote_copy(
            negs.at[slot], negs.at[slot], gsend_sem.at[0, send_slot], grecv_sem.at[0, slot],
            device_id=(peer, o), device_id_type=MESH)

    def copy_term(src_slot, dst_slot, peer):
        return pltpu.make_async_remote_copy(
            term.at[src_slot], term_in.at[dst_slot], gsend_sem.at[1, src_slot], grecv_sem.at[1, dst_slot],
            device_id=(peer, o), device_id_type=MESH)

    for kind in (0, 1):
        @pl.loop(1, owners)
        def _(k):
            peer = xor(o, owners - k, owners)
            copy_in(kind, peer, o, peer).start()

        owned[kind, pl.ds(o, 1)] = sent[kind, pl.ds(o, 1)]

    def wait_in(kind, step):
        for j in range(step_peers):
            src = step * step_peers + j

            @pl.when(src != o)
            def _():
                copy_in(kind, src, src, src).wait_recv()

    def normalized(kind, step):
        values = owned[kind, pl.ds(step * step_peers, step_peers)].astype(f32).reshape(span, width)
        inv = 1.0 / jnp.sqrt(jnp.sum(values * values, axis=1, keepdims=True) + epsilon)
        return values * inv, inv

    def finish(kind, step, grad, unit, inv):
        inner = jnp.sum(unit * grad, axis=1, keepdims=True)
        grad = ((grad - unit * inner) * inv).reshape(step_peers, c, width).astype(bf16)
        stage[kind, pl.ds(step * step_peers, step_peers)] = grad
        for j in range(step_peers):
            peer = step * step_peers + j

            @pl.when(peer != o)
            def _():
                copy_back(kind, peer, o, peer).start()

            @pl.when(peer == o)
            def _():
                back[kind, pl.ds(peer, 1)] = grad[j:j + 1]

    @pl.loop(0, steps)
    def _(k):
        step = xor(my_step, k, steps)
        wait_in(0, step)
        unit, _ = normalized(0, step)
        keys[pl.ds(pl.multiple_of(step * span, span), span)] = unit.astype(bf16)

    choose = (neg_col[...] == lax.broadcasted_iota(jnp.int32, (n_neg, rows), 1)).astype(f32).astype(bf16)
    negs[pl.ds(g, 1)] = dot(choose, keys[:rows]).astype(bf16).reshape(1, n_neg, width)

    @pl.loop(1, groups)
    def _(k):
        peer = xor(g, k, groups)
        copy_neg(g, peer, peer).start()

    @pl.loop(1, groups)
    def _(k):
        peer = xor(g, k, groups)
        copy_neg(peer, peer, peer).wait_recv()

    keys[rows:] = negs[...].astype(f32).reshape(n_all, width).astype(bf16)

    col = lax.broadcasted_iota(jnp.int32, (span, rows + n_all), 1)
    keep = jnp.logical_or(col < rows, (col - rows) // n_neg != g)
    lane = lax.broadcasted_iota(jnp.int32, (span, rows), 1)
    sub = lax.broadcasted_iota(jnp.int32, (span, rows + n_all), 0)
    sub_l = lax.broadcasted_iota(jnp.int32, (span, rows), 0)

    loss_out[...] = jnp.zeros_like(loss_out)

    @pl.loop(0, steps)
    def _(k):
        step = xor(my_step, k, steps)
        row0 = pl.multiple_of(step * span, span)
        wait_in(1, step)
        unit, inv = normalized(1, step)
        half = unit.astype(bf16)
        qh[pl.ds(row0, span)] = half
        s = dot(half, keys[...], ((1,), (1,))) * logit_scale
        e = jnp.where(keep, jnp.exp(s), 0.0)
        denom = jnp.sum(e, axis=1, keepdims=True)
        own = col == sub + row0
        loss = jnp.log(denom) - jnp.sum(jnp.where(own, s, 0.0), axis=1, keepdims=True)
        loss_out[...] += jnp.sum(jnp.where(lane == sub_l + row0, loss, 0.0), axis=0, keepdims=True)
        weight = e / denom - jnp.where(own, 1.0, 0.0)
        coef[pl.ds(row0, span)] = weight.astype(bf16).astype(f32)
        finish(1, step, dot(weight.astype(bf16), keys[...]) * logit_scale, unit, inv)

    coef_t = jnp.transpose(coef[...])
    term[...] = (dot(coef_t[rows:].astype(bf16), qh[...]) * logit_scale).astype(bf16).reshape(groups, n_neg, width)

    @pl.loop(1, groups)
    def _(k):
        peer = xor(g, k, groups)
        copy_term(peer, g, peer).start()

    term_in[pl.ds(g, 1)] = term[pl.ds(g, 1)]
    dp[...] = dot(coef_t[:rows].astype(bf16), qh[...]) * logit_scale

    @pl.loop(1, groups)
    def _(k):
        peer = xor(g, k, groups)
        copy_term(peer, peer, peer).wait_recv()

    which = lax.broadcasted_iota(jnp.int32, (rows, n_neg), 0)
    place = (neg_row[...] == which).astype(f32)
    place = jnp.concatenate([place] * groups, axis=1).astype(bf16)
    terms = term_in[...].astype(f32).reshape(n_all, width).astype(bf16)
    dp[...] += dot(place, terms)

    @pl.loop(0, steps)
    def _(k):
        step = xor(my_step, steps - 1 - k, steps)
        unit, inv = normalized(0, step)
        finish(0, step, dp[pl.ds(pl.multiple_of(step * span, span), span)], unit, inv)

    unpick = (send_row[...] == lax.broadcasted_iota(jnp.int32, (rows, rows), 0)).astype(f32).astype(bf16)
    for kind, out in ((1, q_out), (0, p_out)):
        @pl.loop(1, owners)
        def _(k):
            peer = xor(o, k, owners)
            copy_back(kind, peer, peer, peer).wait_recv()

        out[...] = dot(unpick, back[kind].astype(f32).reshape(rows, width).astype(bf16)).astype(bf16)

    @pl.loop(1, owners)
    def _(k):
        peer = xor(o, k, owners)
        for kind in (0, 1):
            copy_in(kind, peer, o, peer).wait_send()
            copy_back(kind, peer, o, peer).wait_send()

    @pl.loop(1, groups)
    def _(k):
        peer = xor(g, k, groups)
        copy_neg(g, peer, peer).wait_send()
        copy_term(peer, g, peer).wait_send()


def shards(queries, passages, send_order, neg_rows):
    rows, width = queries.shape
    owners, groups = lax.axis_size("owner"), lax.axis_size("group")
    n_neg = neg_rows.shape[1]
    c = rows // owners
    step_peers = min(owners, max(1, 16 // c))
    n_all = groups * n_neg
    vmem = pl.BlockSpec(memory_space=pltpu.VMEM)
    q, p, loss = pl.pallas_call(
        functools.partial(kernel, owners, groups, step_peers),
        out_shape=(
            jax.ShapeDtypeStruct(queries.shape, bf16),
            jax.ShapeDtypeStruct(passages.shape, bf16),
            jax.ShapeDtypeStruct((1, rows), f32),
        ),
        in_specs=[vmem] * 6,
        out_specs=(vmem,) * 3,
        scratch_shapes=[
            pltpu.VMEM((2, owners, c, width), bf16),
            pltpu.VMEM((2, owners, c, width), bf16),
            pltpu.VMEM((rows + n_all, width), bf16),
            pltpu.VMEM((rows, width), bf16),
            pltpu.VMEM((rows, rows + n_all), f32),
            pltpu.VMEM((rows, width), f32),
            pltpu.VMEM((groups, n_neg, width), bf16),
            pltpu.VMEM((groups, n_neg, width), bf16),
            pltpu.VMEM((groups, n_neg, width), bf16),
            pltpu.VMEM((2, owners, c, width), bf16),
            pltpu.VMEM((2, owners, c, width), bf16),
            pltpu.SemaphoreType.DMA((4, owners)),
            pltpu.SemaphoreType.DMA((4, owners)),
            pltpu.SemaphoreType.DMA((2, groups)),
            pltpu.SemaphoreType.DMA((2, groups)),
        ],
        compiler_params=pltpu.CompilerParams(
            collective_id=0, has_side_effects=True, vmem_limit_bytes=48 * 1024 * 1024
        ),
    )(queries, passages, send_order.reshape(rows, 1), send_order, neg_rows.reshape(n_neg, 1), neg_rows)
    return q, p, loss.reshape(rows)


def solution(mesh):
    placed = P(("group", "owner"), None)
    return jax.shard_map(
        shards,
        mesh=mesh,
        in_specs=(placed,) * 4,
        out_specs=(placed, placed, P(("group", "owner"))),
        check_vma=False,
    )
```

```python
import functools

import jax
import jax.numpy as jnp
from jax import lax
from jax.experimental import pallas as pl
from jax.experimental.pallas import tpu as pltpu
from jax.sharding import PartitionSpec as P

logit_scale = 1.0 / 0.05
epsilon = 1e-06
MESH = pl.DeviceIdType.MESH
f32, bf16 = jnp.float32, jnp.bfloat16


def xor(a, b, size):
    out, bit = 0, 1
    while bit < size:
        out = out + ((a // bit + b // bit) % 2) * bit
        bit *= 2
    return out


def dot(a, b, dims=((1,), (0,))):
    return lax.dot_general(a, b, (dims, ((), ())), preferred_element_type=f32)


def unpicked(send_row, values):
    rows = send_row.shape[1]
    unpick = (send_row[...] == lax.broadcasted_iota(jnp.int32, (rows, rows), 0)).astype(f32).astype(bf16)
    return dot(unpick, values.astype(f32).reshape(rows, values.shape[2]).astype(bf16)).astype(bf16)


def place_kernel(parts, q_ref, p_back, loss_ref, send_row, q_hbm, p_hbm, loss_hbm, p_out, sems):
    width = q_ref.shape[1] // parts
    copies = [
        pltpu.make_async_copy(q_ref, q_hbm, sems.at[0]),
        pltpu.make_async_copy(loss_ref, loss_hbm, sems.at[1]),
    ]
    for copy in copies:
        copy.start()
    for i in range(parts):
        cols = pl.ds(i * width, width)
        p_out[:, cols] = unpicked(send_row, p_back[:, :, cols])
        copies.append(pltpu.make_async_copy(p_out.at[:, cols], p_hbm.at[:, cols], sems.at[2 + i]))
        copies[-1].start()
    for copy in copies:
        copy.wait()


def kernel(
    owners, groups, step_peers,
    q_hbm, p_hbm, send_hbm, neg_hbm,
    q_out, p_back, loss_out,
    q_ref, p_ref, send_row, neg_row,
    sent, owned, keys, qh, coef, dp, negs, term, term_in, stage, q_back,
    load_sem, send_sem, recv_sem, gsend_sem, grecv_sem,
):
    rows, width = q_ref.shape
    c = rows // owners
    n_neg = neg_row.shape[1]
    back = (p_back, q_back)
    n_all = groups * n_neg
    steps = owners // step_peers
    span = step_peers * c
    g, o = lax.axis_index("group"), lax.axis_index("owner")
    my_step = o // step_peers

    loads = [
        pltpu.make_async_copy(src, dst, load_sem.at[i])
        for i, (src, dst) in enumerate(
            ((send_hbm, send_row), (p_hbm, p_ref), (q_hbm, q_ref), (neg_hbm, neg_row)))
    ]
    for load in loads:
        load.start()
    barrier = pltpu.get_barrier_semaphore()

    @pl.loop(1, owners)
    def _(k):
        pl.semaphore_signal(barrier, inc=1, device_id=(g, xor(o, k, owners)), device_id_type=MESH)

    @pl.loop(1, groups)
    def _(k):
        pl.semaphore_signal(barrier, inc=1, device_id=(xor(g, k, groups), o), device_id_type=MESH)

    def copy_in(kind, src_slot, dst_slot, peer):
        return pltpu.make_async_remote_copy(
            sent.at[kind, src_slot], owned.at[kind, dst_slot],
            send_sem.at[kind, src_slot], recv_sem.at[kind, dst_slot],
            device_id=(g, peer), device_id_type=MESH)

    def copy_back(kind, src_slot, dst_slot, peer):
        return pltpu.make_async_remote_copy(
            stage.at[kind, src_slot], back[kind].at[dst_slot],
            send_sem.at[2 + kind, src_slot], recv_sem.at[2 + kind, dst_slot],
            device_id=(g, peer), device_id_type=MESH)

    def copy_neg(slot, send_slot, peer):
        return pltpu.make_async_remote_copy(
            negs.at[slot], negs.at[slot], gsend_sem.at[0, send_slot], grecv_sem.at[0, slot],
            device_id=(peer, o), device_id_type=MESH)

    def copy_term(src_slot, dst_slot, peer):
        return pltpu.make_async_remote_copy(
            term.at[src_slot], term_in.at[dst_slot], gsend_sem.at[1, src_slot], grecv_sem.at[1, dst_slot],
            device_id=(peer, o), device_id_type=MESH)

    def column(row_values):
        n = row_values.shape[1]
        square = (n, n)
        diag = lax.broadcasted_iota(jnp.int32, square, 0) == lax.broadcasted_iota(jnp.int32, square, 1)
        return jnp.sum(jnp.where(diag, row_values.astype(f32), 0.0), axis=1, keepdims=True).astype(jnp.int32)

    loads[0].wait()
    pick = (column(send_row[...]) == lax.broadcasted_iota(jnp.int32, (rows, rows), 1)).astype(f32).astype(bf16)
    for kind, source in ((0, p_ref), (1, q_ref)):
        loads[1 + kind].wait()
        sent[kind] = dot(pick, source[...]).reshape(owners, c, width).astype(bf16)
        if kind == 0:
            pl.semaphore_wait(barrier, owners + groups - 2)

        @pl.loop(1, owners)
        def _(k):
            peer = xor(o, k, owners)
            copy_in(kind, peer, o, peer).start()

        owned[kind, pl.ds(o, 1)] = sent[kind, pl.ds(o, 1)]
    loads[3].wait()

    def wait_in(kind, step):
        for j in range(step_peers):
            src = step * step_peers + j

            @pl.when(src != o)
            def _():
                copy_in(kind, src, src, src).wait_recv()

    def normalized(kind, step):
        values = owned[kind, pl.ds(step * step_peers, step_peers)].astype(f32).reshape(span, width)
        inv = 1.0 / jnp.sqrt(jnp.sum(values * values, axis=1, keepdims=True) + epsilon)
        return values * inv, inv

    def finish(kind, step, grad, unit, inv):
        inner = jnp.sum(unit * grad, axis=1, keepdims=True)
        grad = ((grad - unit * inner) * inv).reshape(step_peers, c, width).astype(bf16)
        stage[kind, pl.ds(step * step_peers, step_peers)] = grad
        for j in range(step_peers):
            peer = step * step_peers + j

            @pl.when(peer != o)
            def _():
                copy_back(kind, peer, o, peer).start()

            @pl.when(peer == o)
            def _():
                back[kind][pl.ds(peer, 1)] = grad[j:j + 1]

    @pl.loop(0, steps)
    def _(k):
        step = xor(my_step, k, steps)
        wait_in(0, step)
        unit, _ = normalized(0, step)
        keys[pl.ds(pl.multiple_of(step * span, span), span)] = unit.astype(bf16)

    choose = (column(neg_row[...]) == lax.broadcasted_iota(jnp.int32, (n_neg, rows), 1)).astype(f32).astype(bf16)
    negs[pl.ds(g, 1)] = dot(choose, keys[:rows]).astype(bf16).reshape(1, n_neg, width)

    @pl.loop(1, groups)
    def _(k):
        peer = xor(g, k, groups)
        copy_neg(g, peer, peer).start()

    @pl.loop(1, groups)
    def _(k):
        peer = xor(g, k, groups)
        copy_neg(peer, peer, peer).wait_recv()

    keys[rows:] = negs[...].astype(f32).reshape(n_all, width).astype(bf16)

    col = lax.broadcasted_iota(jnp.int32, (span, rows + n_all), 1)
    keep = jnp.logical_or(col < rows, (col - rows) // n_neg != g)
    lane = lax.broadcasted_iota(jnp.int32, (span, rows), 1)
    sub = lax.broadcasted_iota(jnp.int32, (span, rows + n_all), 0)
    sub_l = lax.broadcasted_iota(jnp.int32, (span, rows), 0)

    loss_out[...] = jnp.zeros_like(loss_out)

    @pl.loop(0, steps)
    def _(k):
        step = xor(my_step, k, steps)
        row0 = pl.multiple_of(step * span, span)
        wait_in(1, step)
        unit, inv = normalized(1, step)
        half = unit.astype(bf16)
        qh[pl.ds(row0, span)] = half
        s = dot(half, keys[...], ((1,), (1,))) * logit_scale
        e = jnp.where(keep, jnp.exp(s), 0.0)
        denom = jnp.sum(e, axis=1, keepdims=True)
        own = col == sub + row0
        loss = jnp.log(denom) - jnp.sum(jnp.where(own, s, 0.0), axis=1, keepdims=True)
        loss_out[...] += jnp.sum(jnp.where(lane == sub_l + row0, loss, 0.0), axis=0, keepdims=True)
        weight = e / denom - jnp.where(own, 1.0, 0.0)
        coef[pl.ds(row0, span)] = weight.astype(bf16).astype(f32)
        finish(1, step, dot(weight.astype(bf16), keys[...]) * logit_scale, unit, inv)

    coef_t = jnp.transpose(coef[...])
    term[...] = (dot(coef_t[rows:].astype(bf16), qh[...]) * logit_scale).astype(bf16).reshape(groups, n_neg, width)

    @pl.loop(1, groups)
    def _(k):
        peer = xor(g, k, groups)
        copy_term(peer, g, peer).start()

    term_in[pl.ds(g, 1)] = term[pl.ds(g, 1)]
    dp[...] = dot(coef_t[:rows].astype(bf16), qh[...]) * logit_scale

    @pl.loop(1, groups)
    def _(k):
        peer = xor(g, k, groups)
        copy_term(peer, peer, peer).wait_recv()

    which = lax.broadcasted_iota(jnp.int32, (span, n_neg), 0)

    @pl.loop(0, steps)
    def _(k):
        step = xor(my_step, (k + steps // 2) % steps, steps)
        row0 = pl.multiple_of(step * span, span)
        place = (neg_row[...] == which + row0).astype(f32)
        place = jnp.concatenate([place] * groups, axis=1).astype(bf16)
        terms = term_in[...].astype(f32).reshape(n_all, width).astype(bf16)
        unit, inv = normalized(0, step)
        finish(0, step, dp[pl.ds(row0, span)] + dot(place, terms), unit, inv)

    for kind in (1, 0):
        @pl.loop(1, owners)
        def _(k):
            peer = xor(o, k, owners)
            copy_back(kind, peer, peer, peer).wait_recv()

        if kind == 1:
            q_out[...] = unpicked(send_row, q_back[...])

    @pl.loop(1, owners)
    def _(k):
        peer = xor(o, k, owners)
        for kind in (0, 1):
            copy_in(kind, peer, o, peer).wait_send()
            copy_back(kind, peer, o, peer).wait_send()

    @pl.loop(1, groups)
    def _(k):
        peer = xor(g, k, groups)
        copy_neg(g, peer, peer).wait_send()
        copy_term(peer, g, peer).wait_send()


def shards(queries, passages, send_order, neg_rows):
    rows, width = queries.shape
    owners, groups = lax.axis_size("owner"), lax.axis_size("group")
    n_neg = neg_rows.shape[1]
    c = rows // owners
    step_peers = min(owners, max(1, 16 // c))
    n_all = groups * n_neg
    vmem = pl.BlockSpec(memory_space=pltpu.VMEM)
    hbm = pl.BlockSpec(memory_space=pltpu.HBM)
    blocks = (owners, c, width)
    neg_blocks = (groups, n_neg, width)
    q_placed, p_back, loss = pl.pallas_call(
        functools.partial(kernel, owners, groups, step_peers),
        out_shape=(
            jax.ShapeDtypeStruct(queries.shape, bf16),
            jax.ShapeDtypeStruct(blocks, bf16),
            jax.ShapeDtypeStruct((1, rows), f32),
        ),
        in_specs=[hbm] * 4,
        out_specs=(vmem,) * 3,
        scratch_shapes=[
            pltpu.VMEM((rows, width), bf16),
            pltpu.VMEM((rows, width), bf16),
            pltpu.VMEM((1, rows), jnp.int32),
            pltpu.VMEM((1, n_neg), jnp.int32),
            pltpu.VMEM((2,) + blocks, bf16),
            pltpu.VMEM((2,) + blocks, bf16),
            pltpu.VMEM((rows + n_all, width), bf16),
            pltpu.VMEM((rows, width), bf16),
            pltpu.VMEM((rows, rows + n_all), f32),
            pltpu.VMEM((rows, width), f32),
            pltpu.VMEM(neg_blocks, bf16),
            pltpu.VMEM(neg_blocks, bf16),
            pltpu.VMEM(neg_blocks, bf16),
            pltpu.VMEM((2,) + blocks, bf16),
            pltpu.VMEM(blocks, bf16),
            pltpu.SemaphoreType.DMA((4,)),
            pltpu.SemaphoreType.DMA((4, owners)),
            pltpu.SemaphoreType.DMA((4, owners)),
            pltpu.SemaphoreType.DMA((2, groups)),
            pltpu.SemaphoreType.DMA((2, groups)),
        ],
        compiler_params=pltpu.CompilerParams(
            collective_id=0, has_side_effects=True, vmem_limit_bytes=67043328
        ),
    )(queries, passages, send_order, neg_rows)
    parts = 2
    q, p, loss = pl.pallas_call(
        functools.partial(place_kernel, parts),
        out_shape=(
            jax.ShapeDtypeStruct(queries.shape, bf16),
            jax.ShapeDtypeStruct(passages.shape, bf16),
            jax.ShapeDtypeStruct((1, rows), f32),
        ),
        in_specs=[vmem] * 4,
        out_specs=(hbm,) * 3,
        scratch_shapes=[pltpu.VMEM((rows, width), bf16), pltpu.SemaphoreType.DMA((2 + parts,))],
        compiler_params=pltpu.CompilerParams(vmem_limit_bytes=8 * 1024 * 1024),
    )(q_placed, p_back, loss, send_order)
    return q, p, loss.reshape(rows)


def solution(mesh):
    placed = P(("group", "owner"), None)
    return jax.shard_map(
        shards,
        mesh=mesh,
        in_specs=(placed,) * 4,
        out_specs=(placed, placed, P(("group", "owner"))),
        check_vma=False,
    )
```

```python
import functools

import jax
import jax.numpy as jnp
from jax import lax
from jax.experimental import pallas as pl
from jax.experimental.pallas import tpu as pltpu
from jax.sharding import PartitionSpec as P

logit_scale = 1.0 / 0.05
epsilon = 1e-06
MESH = pl.DeviceIdType.MESH
f32, bf16 = jnp.float32, jnp.bfloat16


def xor(a, b, size):
    out, bit = 0, 1
    while bit < size:
        out = out + ((a // bit + b // bit) % 2) * bit
        bit *= 2
    return out


def dot(a, b, dims=((1,), (0,))):
    return lax.dot_general(a, b, (dims, ((), ())), preferred_element_type=f32)


def unpicked(send_row, values):
    rows = send_row.shape[1]
    unpick = (send_row[...] == lax.broadcasted_iota(jnp.int32, (rows, rows), 0)).astype(f32).astype(bf16)
    return dot(unpick, values.astype(f32).reshape(rows, values.shape[2]).astype(bf16)).astype(bf16)


def place_kernel(parts, q_in, p_in, loss_in, send_in, q_out, p_out, loss_out, q_ref, p_ref, loss_ref, send_row, p_placed, sems):
    width = q_ref.shape[1] // parts
    spans = [pl.ds(i * width, width) for i in range(parts)]
    pairs = [(send_in, send_row)] + [(p_in.at[:, :, cols], p_ref.at[:, :, cols]) for cols in spans]
    pairs += [(q_in, q_ref), (loss_in, loss_ref)]
    loads = [pltpu.make_async_copy(src, dst, sems.at[0, i]) for i, (src, dst) in enumerate(pairs)]
    pairs = [(p_placed.at[:, cols], p_out.at[:, cols]) for cols in spans] + [(q_ref, q_out), (loss_ref, loss_out)]
    stores = [pltpu.make_async_copy(src, dst, sems.at[1, i]) for i, (src, dst) in enumerate(pairs)]
    for load in loads:
        load.start()
    loads[0].wait()
    for i, cols in enumerate(spans):
        loads[1 + i].wait()
        p_placed[:, cols] = unpicked(send_row, p_ref[:, :, cols])
        stores[i].start()
    for i in (parts, parts + 1):
        loads[1 + i].wait()
        stores[i].start()
    for store in stores:
        store.wait()


def kernel(
    owners, groups, step_peers,
    q_hbm, p_hbm, send_hbm, neg_hbm,
    q_out, p_back, loss_hbm,
    q_ref, p_ref, send_row, neg_row, q_placed, loss_out,
    sent, owned, keys, qh, coef, dp, negs, term, term_in, stage, q_back,
    load_sem, send_sem, recv_sem, gsend_sem, grecv_sem,
):
    rows, width = q_ref.shape
    c = rows // owners
    n_neg = neg_row.shape[1]
    back = (p_back, q_back)
    n_all = groups * n_neg
    steps = owners // step_peers
    span = step_peers * c
    g, o = lax.axis_index("group"), lax.axis_index("owner")
    my_step = o // step_peers

    loads = [
        pltpu.make_async_copy(src, dst, load_sem.at[i])
        for i, (src, dst) in enumerate(
            ((send_hbm, send_row), (p_hbm, p_ref), (q_hbm, q_ref), (neg_hbm, neg_row)))
    ]
    for load in loads:
        load.start()
    barrier = pltpu.get_barrier_semaphore()

    @pl.loop(1, owners)
    def _(k):
        pl.semaphore_signal(barrier, inc=1, device_id=(g, xor(o, k, owners)), device_id_type=MESH)

    @pl.loop(1, groups)
    def _(k):
        pl.semaphore_signal(barrier, inc=1, device_id=(xor(g, k, groups), o), device_id_type=MESH)

    def copy_in(kind, src_slot, dst_slot, peer):
        return pltpu.make_async_remote_copy(
            sent.at[kind, src_slot], owned.at[kind, dst_slot],
            send_sem.at[kind, src_slot], recv_sem.at[kind, dst_slot],
            device_id=(g, peer), device_id_type=MESH)

    def copy_back(kind, src_slot, dst_slot, peer):
        return pltpu.make_async_remote_copy(
            stage.at[kind, src_slot], back[kind].at[dst_slot],
            send_sem.at[2 + kind, src_slot], recv_sem.at[2 + kind, dst_slot],
            device_id=(g, peer), device_id_type=MESH)

    def copy_neg(slot, send_slot, peer):
        return pltpu.make_async_remote_copy(
            negs.at[slot], negs.at[slot], gsend_sem.at[0, send_slot], grecv_sem.at[0, slot],
            device_id=(peer, o), device_id_type=MESH)

    def copy_term(src_slot, dst_slot, peer):
        return pltpu.make_async_remote_copy(
            term.at[src_slot], term_in.at[dst_slot], gsend_sem.at[1, src_slot], grecv_sem.at[1, dst_slot],
            device_id=(peer, o), device_id_type=MESH)

    def column(row_values):
        n = row_values.shape[1]
        square = (n, n)
        diag = lax.broadcasted_iota(jnp.int32, square, 0) == lax.broadcasted_iota(jnp.int32, square, 1)
        return jnp.sum(jnp.where(diag, row_values.astype(f32), 0.0), axis=1, keepdims=True).astype(jnp.int32)

    loads[0].wait()
    pick = (column(send_row[...]) == lax.broadcasted_iota(jnp.int32, (rows, rows), 1)).astype(f32).astype(bf16)
    for kind, source in ((0, p_ref), (1, q_ref)):
        loads[1 + kind].wait()
        sent[kind] = dot(pick, source[...]).reshape(owners, c, width).astype(bf16)
        if kind == 0:
            pl.semaphore_wait(barrier, owners + groups - 2)

        @pl.loop(1, owners)
        def _(k):
            peer = xor(o, k, owners)
            copy_in(kind, peer, o, peer).start()

        owned[kind, pl.ds(o, 1)] = sent[kind, pl.ds(o, 1)]
    loads[3].wait()

    keep_own = pltpu.make_async_copy(stage.at[0, o], p_back.at[o], load_sem.at[4])
    put_q = pltpu.make_async_copy(q_placed, q_out, load_sem.at[5])
    put_loss = pltpu.make_async_copy(loss_out, loss_hbm, load_sem.at[6])

    def wait_in(kind, step):
        for j in range(step_peers):
            src = step * step_peers + j

            @pl.when(src != o)
            def _():
                copy_in(kind, src, src, src).wait_recv()

    def normalized(kind, step):
        values = owned[kind, pl.ds(step * step_peers, step_peers)].astype(f32).reshape(span, width)
        inv = 1.0 / jnp.sqrt(jnp.sum(values * values, axis=1, keepdims=True) + epsilon)
        return values * inv, inv

    def finish(kind, step, grad, unit, inv):
        inner = jnp.sum(unit * grad, axis=1, keepdims=True)
        grad = ((grad - unit * inner) * inv).reshape(step_peers, c, width).astype(bf16)
        stage[kind, pl.ds(step * step_peers, step_peers)] = grad
        for j in range(step_peers):
            peer = step * step_peers + j

            @pl.when(peer != o)
            def _():
                copy_back(kind, peer, o, peer).start()

            @pl.when(peer == o)
            def _():
                if kind == 0:
                    keep_own.start()
                else:
                    q_back[pl.ds(peer, 1)] = grad[j:j + 1]

    @pl.loop(0, steps)
    def _(k):
        step = xor(my_step, k, steps)
        wait_in(0, step)
        unit, _ = normalized(0, step)
        keys[pl.ds(pl.multiple_of(step * span, span), span)] = unit.astype(bf16)

    choose = (column(neg_row[...]) == lax.broadcasted_iota(jnp.int32, (n_neg, rows), 1)).astype(f32).astype(bf16)
    negs[pl.ds(g, 1)] = dot(choose, keys[:rows]).astype(bf16).reshape(1, n_neg, width)

    @pl.loop(1, groups)
    def _(k):
        peer = xor(g, k, groups)
        copy_neg(g, peer, peer).start()

    @pl.loop(1, groups)
    def _(k):
        peer = xor(g, k, groups)
        copy_neg(peer, peer, peer).wait_recv()

    keys[rows:] = negs[...].astype(f32).reshape(n_all, width).astype(bf16)

    col = lax.broadcasted_iota(jnp.int32, (span, rows + n_all), 1)
    keep = jnp.logical_or(col < rows, (col - rows) // n_neg != g)
    lane = lax.broadcasted_iota(jnp.int32, (span, rows), 1)
    sub = lax.broadcasted_iota(jnp.int32, (span, rows + n_all), 0)
    sub_l = lax.broadcasted_iota(jnp.int32, (span, rows), 0)

    loss_out[...] = jnp.zeros_like(loss_out)

    @pl.loop(0, steps)
    def _(k):
        half_way, later = steps // 2, (k + steps - 1) // steps
        step = xor(my_step, half_way * (1 - later) + k - later * (1 - k // (half_way + 1)), steps)
        row0 = pl.multiple_of(step * span, span)
        wait_in(1, step)
        unit, inv = normalized(1, step)
        half = unit.astype(bf16)
        qh[pl.ds(row0, span)] = half
        s = dot(half, keys[...], ((1,), (1,))) * logit_scale
        e = jnp.where(keep, jnp.exp(s), 0.0)
        denom = jnp.sum(e, axis=1, keepdims=True)
        own = col == sub + row0
        loss = jnp.log(denom) - jnp.sum(jnp.where(own, s, 0.0), axis=1, keepdims=True)
        loss_out[...] += jnp.sum(jnp.where(lane == sub_l + row0, loss, 0.0), axis=0, keepdims=True)
        weight = e / denom - jnp.where(own, 1.0, 0.0)
        coef[pl.ds(row0, span)] = weight.astype(bf16).astype(f32)
        finish(1, step, dot(weight.astype(bf16), keys[...]) * logit_scale, unit, inv)

    put_loss.start()
    coef_t = jnp.transpose(coef[...])
    term[...] = (dot(coef_t[rows:].astype(bf16), qh[...]) * logit_scale).astype(bf16).reshape(groups, n_neg, width)

    @pl.loop(1, groups)
    def _(k):
        peer = xor(g, k, groups)
        copy_term(peer, g, peer).start()

    term_in[pl.ds(g, 1)] = term[pl.ds(g, 1)]
    dp[...] = dot(coef_t[:rows].astype(bf16), qh[...]) * logit_scale

    @pl.loop(1, groups)
    def _(k):
        peer = xor(g, k, groups)
        copy_term(peer, peer, peer).wait_recv()

    which = lax.broadcasted_iota(jnp.int32, (span, n_neg), 0)

    @pl.loop(0, steps)
    def _(k):
        step = xor(my_step, (k + steps // 2) % steps, steps)
        row0 = pl.multiple_of(step * span, span)
        place = (neg_row[...] == which + row0).astype(f32)
        place = jnp.concatenate([place] * groups, axis=1).astype(bf16)
        terms = term_in[...].astype(f32).reshape(n_all, width).astype(bf16)
        unit, inv = normalized(0, step)
        finish(0, step, dp[pl.ds(row0, span)] + dot(place, terms), unit, inv)

    for kind in (1, 0):
        @pl.loop(1, owners)
        def _(k):
            peer = xor(o, k, owners)
            copy_back(kind, peer, peer, peer).wait_recv()

        if kind == 1:
            q_placed[...] = unpicked(send_row, q_back[...])
            put_q.start()

    @pl.loop(1, owners)
    def _(k):
        peer = xor(o, k, owners)
        for kind in (0, 1):
            copy_in(kind, peer, o, peer).wait_send()
            copy_back(kind, peer, o, peer).wait_send()

    @pl.loop(1, groups)
    def _(k):
        peer = xor(g, k, groups)
        copy_neg(g, peer, peer).wait_send()
        copy_term(peer, g, peer).wait_send()

    for copy in (keep_own, put_q, put_loss):
        copy.wait()


def shards(queries, passages, send_order, neg_rows):
    rows, width = queries.shape
    owners, groups = lax.axis_size("owner"), lax.axis_size("group")
    n_neg = neg_rows.shape[1]
    c = rows // owners
    step_peers = min(owners, max(1, 16 // c))
    n_all = groups * n_neg
    hbm = pl.BlockSpec(memory_space=pltpu.HBM)
    blocks = (owners, c, width)
    neg_blocks = (groups, n_neg, width)
    q_placed, p_back, loss = pl.pallas_call(
        functools.partial(kernel, owners, groups, step_peers),
        out_shape=(
            jax.ShapeDtypeStruct(queries.shape, bf16),
            jax.ShapeDtypeStruct(blocks, bf16),
            jax.ShapeDtypeStruct((1, rows), f32),
        ),
        in_specs=[hbm] * 4,
        out_specs=(hbm,) * 3,
        scratch_shapes=[
            pltpu.VMEM((rows, width), bf16),
            pltpu.VMEM((rows, width), bf16),
            pltpu.VMEM((1, rows), jnp.int32),
            pltpu.VMEM((1, n_neg), jnp.int32),
            pltpu.VMEM((rows, width), bf16),
            pltpu.VMEM((1, rows), f32),
            pltpu.VMEM((2,) + blocks, bf16),
            pltpu.VMEM((2,) + blocks, bf16),
            pltpu.VMEM((rows + n_all, width), bf16),
            pltpu.VMEM((rows, width), bf16),
            pltpu.VMEM((rows, rows + n_all), f32),
            pltpu.VMEM((rows, width), f32),
            pltpu.VMEM(neg_blocks, bf16),
            pltpu.VMEM(neg_blocks, bf16),
            pltpu.VMEM(neg_blocks, bf16),
            pltpu.VMEM((2,) + blocks, bf16),
            pltpu.VMEM(blocks, bf16),
            pltpu.SemaphoreType.DMA((7,)),
            pltpu.SemaphoreType.DMA((4, owners)),
            pltpu.SemaphoreType.DMA((4, owners)),
            pltpu.SemaphoreType.DMA((2, groups)),
            pltpu.SemaphoreType.DMA((2, groups)),
        ],
        compiler_params=pltpu.CompilerParams(
            collective_id=0, has_side_effects=True, vmem_limit_bytes=67043328
        ),
    )(queries, passages, send_order, neg_rows)
    parts = 2
    q, p, loss = pl.pallas_call(
        functools.partial(place_kernel, parts),
        out_shape=(
            jax.ShapeDtypeStruct(queries.shape, bf16),
            jax.ShapeDtypeStruct(passages.shape, bf16),
            jax.ShapeDtypeStruct((1, rows), f32),
        ),
        in_specs=[hbm] * 4,
        out_specs=(hbm,) * 3,
        scratch_shapes=[
            pltpu.VMEM((rows, width), bf16),
            pltpu.VMEM(blocks, bf16),
            pltpu.VMEM((1, rows), f32),
            pltpu.VMEM((1, rows), jnp.int32),
            pltpu.VMEM((rows, width), bf16),
            pltpu.SemaphoreType.DMA((2, 3 + parts)),
        ],
        compiler_params=pltpu.CompilerParams(vmem_limit_bytes=67043328),
    )(q_placed, p_back, loss, send_order)
    return q, p, loss.reshape(rows)


def solution(mesh):
    placed = P(("group", "owner"), None)
    return jax.shard_map(
        shards,
        mesh=mesh,
        in_specs=(placed,) * 4,
        out_specs=(placed, placed, P(("group", "owner"))),
        check_vma=False,
    )
```

```python
import functools

import jax
import jax.numpy as jnp
from jax import lax
from jax.experimental import pallas as pl
from jax.experimental.pallas import tpu as pltpu
from jax.sharding import PartitionSpec as P

logit_scale = 1.0 / 0.05
epsilon = 1e-06
MESH = pl.DeviceIdType.MESH
f32, bf16 = jnp.float32, jnp.bfloat16


def xor(a, b, size):
    out, bit = 0, 1
    while bit < size:
        out = out + ((a // bit + b // bit) % 2) * bit
        bit *= 2
    return out


def dot(a, b, dims=((1,), (0,))):
    return lax.dot_general(a, b, (dims, ((), ())), preferred_element_type=f32)


def unpicked(send_row, values):
    rows = send_row.shape[1]
    unpick = (send_row[...] == lax.broadcasted_iota(jnp.int32, (rows, rows), 0)).astype(f32).astype(bf16)
    return dot(unpick, values.astype(f32).reshape(rows, values.shape[2]).astype(bf16)).astype(bf16)


def place_kernel(parts, q_in, p_in, loss_in, send_in, q_out, p_out, loss_out, q_ref, p_ref, loss_ref, send_row, p_placed, sems):
    width = q_ref.shape[1] // parts
    spans = [pl.ds(i * width, width) for i in range(parts)]
    pairs = [(send_in, send_row)] + [(p_in.at[:, :, cols], p_ref.at[:, :, cols]) for cols in spans]
    pairs += [(q_in, q_ref), (loss_in, loss_ref)]
    loads = [pltpu.make_async_copy(src, dst, sems.at[0, i]) for i, (src, dst) in enumerate(pairs)]
    pairs = [(p_placed.at[:, cols], p_out.at[:, cols]) for cols in spans] + [(q_ref, q_out), (loss_ref, loss_out)]
    stores = [pltpu.make_async_copy(src, dst, sems.at[1, i]) for i, (src, dst) in enumerate(pairs)]
    for load in loads:
        load.start()
    loads[0].wait()
    for i, cols in enumerate(spans):
        loads[1 + i].wait()
        p_placed[:, cols] = unpicked(send_row, p_ref[:, :, cols])
        stores[i].start()
    for i in (parts, parts + 1):
        loads[1 + i].wait()
        stores[i].start()
    for store in stores:
        store.wait()


def kernel(
    owners, groups, step_peers,
    q_hbm, p_hbm, send_hbm, neg_hbm,
    q_out, p_back, loss_hbm,
    q_ref, p_ref, send_row, neg_row, q_placed, loss_out,
    sent, owned, keys, qh, coef, dp, negs, term, term_in, stage, q_back,
    load_sem, send_sem, recv_sem, gsend_sem, grecv_sem,
):
    rows, width = q_ref.shape
    c = rows // owners
    n_neg = neg_row.shape[1]
    back = (p_back, q_back)
    n_all = groups * n_neg
    steps = owners // step_peers
    span = step_peers * c
    g, o = lax.axis_index("group"), lax.axis_index("owner")
    my_step = o // step_peers

    loads = [
        pltpu.make_async_copy(src, dst, load_sem.at[i])
        for i, (src, dst) in enumerate(
            ((send_hbm, send_row), (p_hbm, p_ref), (q_hbm, q_ref), (neg_hbm, neg_row)))
    ]
    for load in loads:
        load.start()
    barrier = pltpu.get_barrier_semaphore()

    @pl.loop(1, owners)
    def _(k):
        pl.semaphore_signal(barrier, inc=1, device_id=(g, xor(o, k, owners)), device_id_type=MESH)

    @pl.loop(1, groups)
    def _(k):
        pl.semaphore_signal(barrier, inc=1, device_id=(xor(g, k, groups), o), device_id_type=MESH)

    def copy_in(kind, src_slot, dst_slot, peer):
        return pltpu.make_async_remote_copy(
            sent.at[kind, src_slot], owned.at[kind, dst_slot],
            send_sem.at[kind, src_slot], recv_sem.at[kind, dst_slot],
            device_id=(g, peer), device_id_type=MESH)

    def copy_back(kind, src_slot, dst_slot, peer):
        return pltpu.make_async_remote_copy(
            stage.at[kind, src_slot], back[kind].at[dst_slot],
            send_sem.at[2 + kind, src_slot], recv_sem.at[2 + kind, dst_slot],
            device_id=(g, peer), device_id_type=MESH)

    def copy_neg(slot, send_slot, peer):
        return pltpu.make_async_remote_copy(
            negs.at[slot], negs.at[slot], gsend_sem.at[0, send_slot], grecv_sem.at[0, slot],
            device_id=(peer, o), device_id_type=MESH)

    def copy_term(src_slot, dst_slot, peer):
        return pltpu.make_async_remote_copy(
            term.at[src_slot], term_in.at[dst_slot], gsend_sem.at[1, src_slot], grecv_sem.at[1, dst_slot],
            device_id=(peer, o), device_id_type=MESH)

    def column(row_values):
        n = row_values.shape[1]
        square = (n, n)
        diag = lax.broadcasted_iota(jnp.int32, square, 0) == lax.broadcasted_iota(jnp.int32, square, 1)
        return jnp.sum(jnp.where(diag, row_values.astype(f32), 0.0), axis=1, keepdims=True).astype(jnp.int32)

    loads[0].wait()
    pick = (column(send_row[...]) == lax.broadcasted_iota(jnp.int32, (rows, rows), 1)).astype(f32).astype(bf16)
    for kind, source in ((0, p_ref), (1, q_ref)):
        loads[1 + kind].wait()
        sent[kind] = dot(pick, source[...]).reshape(owners, c, width).astype(bf16)
        if kind == 0:
            pl.semaphore_wait(barrier, owners + groups - 2)

        @pl.loop(1, owners)
        def _(k):
            peer = xor(o, owners - k, owners)
            copy_in(kind, peer, o, peer).start()

        owned[kind, pl.ds(o, 1)] = sent[kind, pl.ds(o, 1)]
    loads[3].wait()

    keep_own = pltpu.make_async_copy(stage.at[0, o], p_back.at[o], load_sem.at[4])
    put_q = pltpu.make_async_copy(q_placed, q_out, load_sem.at[5])
    put_loss = pltpu.make_async_copy(loss_out, loss_hbm, load_sem.at[6])

    def wait_in(kind, step):
        for j in range(step_peers):
            src = step * step_peers + j

            @pl.when(src != o)
            def _():
                copy_in(kind, src, src, src).wait_recv()

    def normalized(kind, step):
        values = owned[kind, pl.ds(step * step_peers, step_peers)].astype(f32).reshape(span, width)
        inv = 1.0 / jnp.sqrt(jnp.sum(values * values, axis=1, keepdims=True) + epsilon)
        return values * inv, inv

    def finish(kind, step, grad, unit, inv):
        inner = jnp.sum(unit * grad, axis=1, keepdims=True)
        grad = ((grad - unit * inner) * inv).reshape(step_peers, c, width).astype(bf16)
        stage[kind, pl.ds(step * step_peers, step_peers)] = grad
        for j in range(step_peers):
            peer = step * step_peers + j

            @pl.when(peer != o)
            def _():
                copy_back(kind, peer, o, peer).start()

            @pl.when(peer == o)
            def _():
                if kind == 0:
                    keep_own.start()
                else:
                    q_back[pl.ds(peer, 1)] = grad[j:j + 1]

    @pl.loop(0, steps)
    def _(k):
        step = xor(my_step, k, steps)
        wait_in(0, step)
        unit, _ = normalized(0, step)
        keys[pl.ds(pl.multiple_of(step * span, span), span)] = unit.astype(bf16)

    choose = (column(neg_row[...]) == lax.broadcasted_iota(jnp.int32, (n_neg, rows), 1)).astype(f32).astype(bf16)
    negs[pl.ds(g, 1)] = dot(choose, keys[:rows]).astype(bf16).reshape(1, n_neg, width)

    @pl.loop(1, groups)
    def _(k):
        peer = xor(g, k, groups)
        copy_neg(g, peer, peer).start()

    @pl.loop(1, groups)
    def _(k):
        peer = xor(g, k, groups)
        copy_neg(peer, peer, peer).wait_recv()

    keys[rows:] = negs[...].astype(f32).reshape(n_all, width).astype(bf16)

    col = lax.broadcasted_iota(jnp.int32, (span, rows + n_all), 1)
    keep = jnp.logical_or(col < rows, (col - rows) // n_neg != g)
    lane = lax.broadcasted_iota(jnp.int32, (span, rows), 1)
    sub = lax.broadcasted_iota(jnp.int32, (span, rows + n_all), 0)
    sub_l = lax.broadcasted_iota(jnp.int32, (span, rows), 0)

    loss_out[...] = jnp.zeros_like(loss_out)

    @pl.loop(0, steps)
    def _(k):
        step = xor(my_step, k, steps)
        row0 = pl.multiple_of(step * span, span)
        wait_in(1, step)
        unit, inv = normalized(1, step)
        half = unit.astype(bf16)
        qh[pl.ds(row0, span)] = half
        s = dot(half, keys[...], ((1,), (1,))) * logit_scale
        e = jnp.where(keep, jnp.exp(s), 0.0)
        denom = jnp.sum(e, axis=1, keepdims=True)
        own = col == sub + row0
        loss = jnp.log(denom) - jnp.sum(jnp.where(own, s, 0.0), axis=1, keepdims=True)
        loss_out[...] += jnp.sum(jnp.where(lane == sub_l + row0, loss, 0.0), axis=0, keepdims=True)
        weight = e / denom - jnp.where(own, 1.0, 0.0)
        coef[pl.ds(row0, span)] = weight.astype(bf16).astype(f32)
        finish(1, step, dot(weight.astype(bf16), keys[...]) * logit_scale, unit, inv)

    put_loss.start()
    coef_t = jnp.transpose(coef[...])
    term[...] = (dot(coef_t[rows:].astype(bf16), qh[...]) * logit_scale).astype(bf16).reshape(groups, n_neg, width)

    @pl.loop(1, groups)
    def _(k):
        peer = xor(g, k, groups)
        copy_term(peer, g, peer).start()

    term_in[pl.ds(g, 1)] = term[pl.ds(g, 1)]
    dp[...] = dot(coef_t[:rows].astype(bf16), qh[...]) * logit_scale

    @pl.loop(1, groups)
    def _(k):
        peer = xor(g, k, groups)
        copy_term(peer, peer, peer).wait_recv()

    which = lax.broadcasted_iota(jnp.int32, (span, n_neg), 0)

    @pl.loop(0, steps)
    def _(k):
        step = xor(my_step, (k + steps // 2) % steps, steps)
        row0 = pl.multiple_of(step * span, span)
        place = (neg_row[...] == which + row0).astype(f32)
        place = jnp.concatenate([place] * groups, axis=1).astype(bf16)
        terms = term_in[...].astype(f32).reshape(n_all, width).astype(bf16)
        unit, inv = normalized(0, step)
        finish(0, step, dp[pl.ds(row0, span)] + dot(place, terms), unit, inv)

    for kind in (1, 0):
        @pl.loop(1, owners)
        def _(k):
            peer = xor(o, k, owners)
            copy_back(kind, peer, peer, peer).wait_recv()

        if kind == 1:
            q_placed[...] = unpicked(send_row, q_back[...])
            put_q.start()

    @pl.loop(1, owners)
    def _(k):
        peer = xor(o, k, owners)
        for kind in (0, 1):
            copy_in(kind, peer, o, peer).wait_send()
            copy_back(kind, peer, o, peer).wait_send()

    @pl.loop(1, groups)
    def _(k):
        peer = xor(g, k, groups)
        copy_neg(g, peer, peer).wait_send()
        copy_term(peer, g, peer).wait_send()

    for copy in (keep_own, put_q, put_loss):
        copy.wait()


def shards(queries, passages, send_order, neg_rows):
    rows, width = queries.shape
    owners, groups = lax.axis_size("owner"), lax.axis_size("group")
    n_neg = neg_rows.shape[1]
    c = rows // owners
    step_peers = min(owners, max(1, 16 // c))
    n_all = groups * n_neg
    hbm = pl.BlockSpec(memory_space=pltpu.HBM)
    blocks = (owners, c, width)
    neg_blocks = (groups, n_neg, width)
    q_placed, p_back, loss = pl.pallas_call(
        functools.partial(kernel, owners, groups, step_peers),
        out_shape=(
            jax.ShapeDtypeStruct(queries.shape, bf16),
            jax.ShapeDtypeStruct(blocks, bf16),
            jax.ShapeDtypeStruct((1, rows), f32),
        ),
        in_specs=[hbm] * 4,
        out_specs=(hbm,) * 3,
        scratch_shapes=[
            pltpu.VMEM((rows, width), bf16),
            pltpu.VMEM((rows, width), bf16),
            pltpu.VMEM((1, rows), jnp.int32),
            pltpu.VMEM((1, n_neg), jnp.int32),
            pltpu.VMEM((rows, width), bf16),
            pltpu.VMEM((1, rows), f32),
            pltpu.VMEM((2,) + blocks, bf16),
            pltpu.VMEM((2,) + blocks, bf16),
            pltpu.VMEM((rows + n_all, width), bf16),
            pltpu.VMEM((rows, width), bf16),
            pltpu.VMEM((rows, rows + n_all), f32),
            pltpu.VMEM((rows, width), f32),
            pltpu.VMEM(neg_blocks, bf16),
            pltpu.VMEM(neg_blocks, bf16),
            pltpu.VMEM(neg_blocks, bf16),
            pltpu.VMEM((2,) + blocks, bf16),
            pltpu.VMEM(blocks, bf16),
            pltpu.SemaphoreType.DMA((7,)),
            pltpu.SemaphoreType.DMA((4, owners)),
            pltpu.SemaphoreType.DMA((4, owners)),
            pltpu.SemaphoreType.DMA((2, groups)),
            pltpu.SemaphoreType.DMA((2, groups)),
        ],
        compiler_params=pltpu.CompilerParams(
            collective_id=0, has_side_effects=True, vmem_limit_bytes=67043328
        ),
    )(queries, passages, send_order, neg_rows)
    parts = 2
    q, p, loss = pl.pallas_call(
        functools.partial(place_kernel, parts),
        out_shape=(
            jax.ShapeDtypeStruct(queries.shape, bf16),
            jax.ShapeDtypeStruct(passages.shape, bf16),
            jax.ShapeDtypeStruct((1, rows), f32),
        ),
        in_specs=[hbm] * 4,
        out_specs=(hbm,) * 3,
        scratch_shapes=[
            pltpu.VMEM((rows, width), bf16),
            pltpu.VMEM(blocks, bf16),
            pltpu.VMEM((1, rows), f32),
            pltpu.VMEM((1, rows), jnp.int32),
            pltpu.VMEM((rows, width), bf16),
            pltpu.SemaphoreType.DMA((2, 3 + parts)),
        ],
        compiler_params=pltpu.CompilerParams(vmem_limit_bytes=67043328),
    )(q_placed, p_back, loss, send_order)
    return q, p, loss.reshape(rows)


def solution(mesh):
    placed = P(("group", "owner"), None)
    return jax.shard_map(
        shards,
        mesh=mesh,
        in_specs=(placed,) * 4,
        out_specs=(placed, placed, P(("group", "owner"))),
        check_vma=False,
    )
```
